768 devices in a mesh: occ: 16 (over y, x_hi), vir: 48 (over z, x_lo, core).
Axes of the slice: x: 4 (x_hi: 2, x_lo: 2; x = x_hi * 2 + x_lo), y: 8, z: 12, core: 2. Of those that a mesh axis runs over, the one named last changes fastest.
Arguments:
- amplitudes: bfloat16 [32, 32, 768, 768], P('occ', None, 'vir'), may hold values from -6 to 6
- integrals: bfloat16 [768, 768], P('vir'), may hold values from -0.21875 to 0.21875
- occ_fock: bfloat16 [32, 32], replicated, may hold values from -1 to 1
- amp_mask: int32 [48, 48], replicated, may hold values 0 or 1
- int_mask: int32 [48, 48], replicated, may hold values 0 or 1
- occ_energy: float32 [32], replicated, may hold values from -2 to -0.5
- vir_energy: float32 [768], replicated, may hold values from 0.5 to 4
Outputs:
- update: float32 [32, 32, 768, 768], P('occ', None, 'vir')
The draws below stay inside these ranges and needn't reach their ends.
All inputs are finite; a program needn't handle non-finite values.
Results may differ from the reference program's by a relative error of at most 0.002.
Values may be sent and summed in bfloat16 or wider, within the bound.
A program may use at most 128 MiB of HBM per device.

```python
import jax
import jax.numpy as jnp
from jax import lax

V = 768
VB = 16
NO = 32
NVB = 48


def plant(values, stream_key, least, high):
    place = [jax.random.randint(jax.random.fold_in(stream_key, axis), (), 0, length) for axis, length in enumerate(values.shape)]
    main_axis = values.shape.index(max(values.shape))
    next_to = place[:main_axis] + [(place[main_axis] + 1) % values.shape[main_axis]] + place[main_axis + 1:]
    return values.at[tuple(place)].set(least).at[tuple(next_to)].set(high)


def shard_levels(key, dims, cuts, low, top_value):
    factor_of = 1.0
    for dim, blocks in cuts:
        heights = jax.random.uniform(jax.random.fold_in(jax.random.fold_in(key, 6), dim), (blocks,), jnp.float32, low / len(cuts), top_value / len(cuts))
        factor_of = factor_of * jnp.repeat(jnp.exp(heights), dims[dim] // blocks).reshape((-1,) + (1,) * (len(dims) - 1 - dim))
    return factor_of


def centred(key, dims, scale, limit, shards=(), kind=jnp.bfloat16):
    drawn = jax.random.normal(key, dims, jnp.float32) * scale
    if len(shards) > 0:
        drawn = shard_levels(key, dims, shards, -0.22, 0.18) * drawn
    return jnp.clip(drawn, min=-limit, max=limit).astype(kind)


def setup_inputs(seed: int = 0) -> dict:
    key_list = jax.random.split(jax.random.key(seed), 8)
    amplitudes = centred(key_list[0], (NO, NO, V, V), 1.0, 6.0, ((0, 16), (2, 48)))
    integrals = centred(key_list[1], (V, V), V ** -0.5, 0.21875, ((0, 48),))
    occ_fock = centred(key_list[2], (NO, NO), NO ** -0.5, 1.0)
    amp_mask = plant((jax.random.randint(key_list[3], (NVB, NVB), 0, 4) < 3).astype(jnp.int32), jax.random.fold_in(key_list[3], 1), 0, 1)
    int_mask = plant((jax.random.randint(key_list[4], (NVB, NVB), 0, 2) < 1).astype(jnp.int32), jax.random.fold_in(key_list[4], 1), 0, 1)
    occ_energy = jnp.clip(jax.random.uniform(key_list[5], (NO,), jnp.float32, -2.0, -0.5), -2.0, -0.5)
    vir_energy = jnp.clip(jax.random.uniform(key_list[6], (V,), jnp.float32, 0.5, 4.0), 0.5, 4.0)
    return dict(amplitudes=amplitudes, integrals=integrals, occ_fock=occ_fock, amp_mask=amp_mask, int_mask=int_mask, occ_energy=occ_energy, vir_energy=vir_energy)


def expand(mask):
    return jnp.repeat(jnp.repeat(mask, VB, axis=0), VB, axis=1).astype(jnp.bfloat16)


def reference(amplitudes, integrals, occ_fock, amp_mask, int_mask, occ_energy, vir_energy):
    amp_tiles = expand(amp_mask)
    masked_w = integrals * expand(int_mask)
    fock_wide = occ_fock.astype(jnp.float32)

    def one_row(index):
        tile = amplitudes[index] * amp_tiles[None]
        ladder = jnp.dot(tile.reshape(-1, V), masked_w, preferred_element_type=jnp.float32).reshape(NO, V, V)
        holes = jnp.einsum("kab,kj->jab", tile.astype(jnp.float32), fock_wide)
        return ladder + holes

    mixed = lax.map(one_row, jnp.arange(NO))

    def finish(index):
        narrow = mixed[:, index].astype(jnp.bfloat16)
        narrow = lax.optimization_barrier(narrow)
        mirror = narrow.astype(jnp.float32).transpose(0, 2, 1)
        denom = vir_energy[None, :, None] + vir_energy[None, None, :] - occ_energy[index] - occ_energy[:, None, None]
        return (mixed[index] + mirror) / denom

    return lax.map(finish, jnp.arange(NO))
```

```python
import jax
import jax.numpy as jnp
from jax import lax
from jax.experimental import pallas as pl
from jax.experimental.pallas import tpu as pltpu
from jax.sharding import PartitionSpec as P

VB = 16
NO = 32
V = 768
N_OCC = 16
N_VIR = 48
N_Z = 12
N_DEV = N_OCC * N_VIR
MESH = pl.DeviceIdType.MESH
F32, BF16 = jnp.float32, jnp.bfloat16
ANY = pl.BlockSpec(memory_space=pl.ANY)
IN_VMEM = pl.BlockSpec(memory_space=pltpu.VMEM)
IN_SMEM = pl.BlockSpec(memory_space=pltpu.SMEM)

Z_ORDER = (1, 11, 2, 10, 3, 9, 4, 8, 5, 7, 6)


def gather_kernel(w_ref, full_ref, own_sem, z_send, z_recv, x_send, x_recv, c_send, c_recv, d_send, d_recv):
    me = lax.axis_index("vir")
    z, x, c = me // 4, (me // 2) % 2, me % 2
    x_peer, c_peer = z * 4 + (1 - x) * 2 + c, z * 4 + x * 2 + (1 - c)

    barrier = pltpu.get_barrier_semaphore()
    for dz in Z_ORDER:
        pl.semaphore_signal(barrier, inc=1, device_id={"vir": ((z + dz) % N_Z) * 4 + x * 2 + c}, device_id_type=MESH)
    for peer in (x_peer, c_peer):
        pl.semaphore_signal(barrier, inc=1, device_id={"vir": peer}, device_id_type=MESH)
    pl.semaphore_wait(barrier, N_Z + 1)

    def send(src, slot, send_sem, recv_sem, peer):
        return pltpu.make_async_remote_copy(
            src_ref=src, dst_ref=full_ref.at[slot], send_sem=send_sem, recv_sem=recv_sem,
            device_id={"vir": peer}, device_id_type=MESH)

    sends = []

    def go(copy):
        copy.start()
        sends.append(copy)

    own = pltpu.make_async_copy(w_ref, full_ref.at[me], own_sem)
    own.start()
    for dz in Z_ORDER:
        go(send(w_ref, me, z_send.at[dz], z_recv.at[dz], ((z + dz) % N_Z) * 4 + x * 2 + c))
    go(send(w_ref, me, x_send.at[0], x_recv.at[0], x_peer))
    go(send(w_ref, me, c_send.at[0], c_recv.at[0], c_peer))

    def from_x(dz):
        slot = ((z - dz + N_Z) % N_Z) * 4 + (1 - x) * 2 + c
        send(full_ref.at[slot], slot, x_send.at[dz], x_recv.at[dz], x_peer).wait_recv()
        go(send(full_ref.at[slot], slot, d_send.at[dz], d_recv.at[dz], c_peer))

    before = 0
    for dz in Z_ORDER:
        slot = ((z - dz + N_Z) % N_Z) * 4 + x * 2 + c
        send(full_ref.at[slot], slot, z_send.at[dz], z_recv.at[dz], x_peer).wait_recv()
        go(send(full_ref.at[slot], slot, x_send.at[dz], x_recv.at[dz], x_peer))
        go(send(full_ref.at[slot], slot, c_send.at[dz], c_recv.at[dz], c_peer))
        from_x(before)
        before = dz
    from_x(before)
    for dz in range(N_Z):
        slot = ((z - dz + N_Z) % N_Z) * 4 + x * 2 + (1 - c)
        send(full_ref.at[slot], slot, c_send.at[dz], c_recv.at[dz], c_peer).wait_recv()
        slot = ((z - dz + N_Z) % N_Z) * 4 + (1 - x) * 2 + (1 - c)
        send(full_ref.at[slot], slot, d_send.at[dz], d_recv.at[dz], c_peer).wait_recv()
    for copy in sends:
        copy.wait_send()
    own.wait()


def gather(w):
    rows, cols = w.shape
    sem = pltpu.SemaphoreType.DMA((N_Z,))
    return pl.pallas_call(
        gather_kernel,
        out_shape=jax.ShapeDtypeStruct((N_VIR, rows, cols), w.dtype),
        in_specs=[IN_VMEM],
        out_specs=IN_VMEM,
        scratch_shapes=[pltpu.SemaphoreType.DMA] + [sem] * 8,
        compiler_params=pltpu.CompilerParams(collective_id=0, has_side_effects=True),
        name="gather_w",
    )(w)


def one_hot(rows, cols, hit):
    r = lax.broadcasted_iota(jnp.int32, (rows, cols), 0)
    c = lax.broadcasted_iota(jnp.int32, (rows, cols), 1)
    return jnp.where(hit(r, c), 1.0, 0.0).astype(BF16)


COLS = 256


def mix_kernel(amps_ref, w_ref, g_ref, amask_ref, imask_ref, mixed_ref, out_ref, masked, holes):
    me = lax.axis_index("vir")
    wide = one_hot(N_VIR, V, lambda r, c: r == c // VB)
    tall = one_hot(V, N_VIR, lambda r, c: r // VB == c)
    row = amask_ref[pl.ds(me, 1), :].astype(F32).astype(BF16)
    keep = jnp.dot(jnp.broadcast_to(row, (8, N_VIR)), wide, preferred_element_type=F32)[:1].astype(BF16)

    def mask_one(n, carry):
        i, j = n // NO, n % NO
        masked[i, pl.ds(j * VB, VB), :] = amps_ref[i, j] * keep
        return carry

    lax.fori_loop(0, 2 * NO, mask_one, 0, unroll=8)

    spread = one_hot(NO, NO * VB, lambda r, c: r == c // VB)
    g_wide = lax.dot_general(g_ref[...], spread, (((0,), (0,)), ((), ())), preferred_element_type=F32).astype(BF16)
    pick = one_hot(NO * VB, NO, lambda r, c: r // VB == c)
    kron = jnp.dot(pick, g_wide, preferred_element_type=F32)
    same = lax.broadcasted_iota(jnp.int32, kron.shape, 0) % VB == lax.broadcasted_iota(jnp.int32, kron.shape, 1) % VB
    holes[...] = jnp.where(same, kron, 0.0).astype(BF16)

    imask = imask_ref[...].astype(F32).astype(BF16)
    tall_mask = jnp.dot(tall, imask, preferred_element_type=F32).astype(BF16)
    for n in range(V // COLS):
        cols = slice(n * COLS, (n + 1) * COLS)
        w_keep = jnp.dot(tall_mask, wide[:, cols], preferred_element_type=F32).astype(BF16)
        w = w_ref[:, cols] * w_keep

        def rows_of(i, carry):
            both = jnp.dot(masked[i], w, preferred_element_type=F32)
            both = both + jnp.dot(holes[...], masked[i, :, cols], preferred_element_type=F32)
            mixed_ref[i, :, :, cols] = both.reshape(NO, VB, COLS)
            return carry

        lax.fori_loop(0, 2, rows_of, 0)

    low = lax.broadcasted_iota(jnp.int32, (N_VIR, 8, 128), 2) < 64

    def pack(p, carry):
        slabs = [mixed_ref[i, pl.ds(4 * p + 2 * h, 2)].reshape(2 * VB, V) for h in (0, 1) for i in (0, 1)]
        turned = jnp.concatenate(slabs, axis=0).T.reshape(N_VIR, 2, 8, 128)
        top, bottom = turned[:, 0], turned[:, 1]
        out_ref[2 * p] = jnp.where(low, top, pltpu.roll(bottom, 64, 2)).astype(BF16)
        out_ref[2 * p + 1] = jnp.where(low, pltpu.roll(top, 64, 2), bottom).astype(BF16)
        return carry

    lax.fori_loop(0, N_OCC // 2, pack, 0)


def mix(amps, w, g, amask, imask):
    return pl.pallas_call(
        mix_kernel,
        out_shape=(
            jax.ShapeDtypeStruct((2, NO, VB, V), F32),
            jax.ShapeDtypeStruct((N_OCC, N_VIR, 8, 128), BF16),
        ),
        in_specs=[IN_VMEM] * 5,
        out_specs=(IN_VMEM, IN_VMEM),
        scratch_shapes=[pltpu.VMEM((2, NO * VB, V), BF16), pltpu.VMEM((NO * VB, NO * VB), BF16)],
        compiler_params=pltpu.CompilerParams(vmem_limit_bytes=48 * 2**20),
        name="mix",
    )(amps, w, g, amask, imask)


def exchange_kernel(x_ref, o_ref, own_sem, send_sem, recv_sem):
    occ, vir = lax.axis_index("occ"), lax.axis_index("vir")
    me = occ * N_VIR + vir
    own = pltpu.make_async_copy(x_ref.at[me], o_ref.at[me], own_sem)
    own.start()

    def send(s, carry):
        to_occ = lax.rem(occ + s % N_OCC, N_OCC)
        to_vir = lax.rem(vir + ((s // N_OCC) * 19 + s * 7) % N_VIR, N_VIR)
        pltpu.make_async_remote_copy(
            src_ref=x_ref.at[to_occ * N_VIR + to_vir], dst_ref=o_ref.at[me], send_sem=send_sem, recv_sem=recv_sem,
            device_id=(to_occ, to_vir), device_id_type=MESH).start()
        return carry

    lax.fori_loop(1, N_DEV, send, 0)
    others = pl.ds(0, N_DEV - 1)
    pltpu.make_async_copy(x_ref.at[others], o_ref.at[others], recv_sem).wait()
    pltpu.make_async_copy(x_ref.at[others], o_ref.at[others], send_sem).wait()
    own.wait()


def exchange(tiles):
    return pl.pallas_call(
        exchange_kernel,
        out_shape=jax.ShapeDtypeStruct((N_DEV, 8, 128), BF16),
        in_specs=[IN_VMEM],
        out_specs=IN_VMEM,
        scratch_shapes=[pltpu.SemaphoreType.DMA] * 3,
        compiler_params=pltpu.CompilerParams(has_side_effects=True),
        name="exchange",
    )(tiles)


def finish_kernel(tiles_ref, mixed_ref, vir_sum_ref, occ_ref, out_ref):
    source = pl.program_id(0)
    occ = lax.axis_index("occ")
    x = tiles_ref[...].astype(F32).reshape(N_VIR // 8, 8, 8, 128)
    parts = [x[:, t] for t in range(8)]
    chunk = lax.broadcasted_iota(jnp.int32, parts[0].shape, 2) // VB
    for k in (1, 2, 4):
        low = (chunk // k) % 2 == 0
        for t in range(8):
            if t & k == 0:
                a, b = parts[t], parts[t + k]
                parts[t] = jnp.where(low, a, pltpu.roll(b, VB * k, 2))
                parts[t + k] = jnp.where(low, pltpu.roll(a, 128 - VB * k, 2), b)
    for c in range(8):
        half, i, jj = c // 4, (c // 2) % 2, c % 2
        energy = occ_ref[2 * occ + jj] + occ_ref[2 * source + i]
        rows = slice(half * 8, half * 8 + 8)
        for g in range(N_VIR // 8):
            cols = slice(g * 128, g * 128 + 128)
            total = mixed_ref[jj, i, rows, cols] + parts[c][g]
            out_ref[jj, i, rows, cols] = total / (vir_sum_ref[rows, cols] - energy)


def finish(tiles, mixed, vir_sum, occ_energy):
    block = pl.BlockSpec((2, 2, VB, V), lambda s: (0, s, 0, 0))
    return pl.pallas_call(
        finish_kernel,
        out_shape=jax.ShapeDtypeStruct((2, NO, VB, V), F32),
        grid=(N_OCC,),
        in_specs=[
            pl.BlockSpec((N_VIR, 8, 128), lambda s: (s, 0, 0)),
            block,
            pl.BlockSpec((VB, V), lambda s: (0, 0)),
            IN_SMEM,
        ],
        out_specs=block,
        name="finish",
    )(tiles, mixed, vir_sum, occ_energy)


def local(amplitudes, integrals, occ_fock, amp_mask, int_mask, occ_energy, vir_energy):
    vir_here = lax.dynamic_slice_in_dim(vir_energy, lax.axis_index("vir") * VB, VB, 0)
    vir_sum = vir_here[:, None] + vir_energy[None, :]
    full_w = gather(integrals).reshape(V, V)
    mixed, outgoing = mix(amplitudes, full_w, occ_fock, amp_mask, int_mask)
    arrived = exchange(outgoing.reshape(N_DEV, 8, 128))
    return finish(arrived, mixed, vir_sum, occ_energy)


def solution(mesh):
    in_specs = (P("occ", None, "vir", None), P("vir", None), P(), P(), P(), P(), P())
    out_specs = P("occ", None, "vir", None)
    return jax.shard_map(local, mesh=mesh, in_specs=in_specs, out_specs=out_specs, check_vma=False)
```

```python
import jax
import jax.numpy as jnp
from jax import lax
from jax.experimental import pallas as pl
from jax.experimental.pallas import tpu as pltpu
from jax.sharding import PartitionSpec as P

VB = 16
NO = 32
V = 768
N_OCC = 16
N_VIR = 48
N_Z = 12
N_DEV = N_OCC * N_VIR
N_PAIR = N_Z // 2
ROWS = NO * VB
MESH = pl.DeviceIdType.MESH
F32, BF16 = jnp.float32, jnp.bfloat16
IN_HBM = pl.BlockSpec(memory_space=pltpu.HBM)
IN_VMEM = pl.BlockSpec(memory_space=pltpu.VMEM)

Z_ORDER = (1, 11, 2, 10, 3, 9, 4, 8, 5, 7, 6)
PAIR_ORDER = ((3,), (2, 4), (1, 5), (0,))


def one_hot(rows, cols, hit):
    r = lax.broadcasted_iota(jnp.int32, (rows, cols), 0)
    c = lax.broadcasted_iota(jnp.int32, (rows, cols), 1)
    return jnp.where(hit(r, c), 1.0, 0.0).astype(BF16)


def kernel(
    amps_hbm, w_hbm, g_hbm, amask_hbm, imask_hbm, num_ref,
    amps, g, amask, imask, full, masked, holes, tall_mask, tiles, arrived,
    in_sem, z_send, z_recv, x_send, x_recv, c_send, c_recv, d_send, d_recv, entered, out_sem, tile_sem, own_sem,
):
    occ, me = lax.axis_index("occ"), lax.axis_index("vir")
    flat = occ * N_VIR + me
    z, x, c = me // 4, (me // 2) % 2, me % 2
    zp, odd = z // 2, z % 2
    x_peer, c_peer = z * 4 + (1 - x) * 2 + c, z * 4 + x * 2 + (1 - c)

    pairs = ((w_hbm, full.at[me]), (amps_hbm, amps), (amask_hbm, amask), (g_hbm, g), (imask_hbm, imask))
    loads = [pltpu.make_async_copy(src, dst, in_sem.at[n]) for n, (src, dst) in enumerate(pairs)]
    for load in loads:
        load.start()

    barrier = pltpu.get_barrier_semaphore()

    def greet_vir(s, carry):
        pl.semaphore_signal(barrier, inc=1, device_id=(occ, (me + s) % N_VIR), device_id_type=MESH)
        return carry

    def greet_occ(s, carry):
        pl.semaphore_signal(barrier, inc=1, device_id=((occ + s) % N_OCC, me), device_id_type=MESH)
        return carry

    def pass_on(s, carry):
        pl.semaphore_signal(entered, inc=1, device_id=((occ + s) % N_OCC, me), device_id_type=MESH)
        return carry

    lax.fori_loop(1, N_VIR, greet_vir, 0)
    lax.fori_loop(1, N_OCC, greet_occ, 0)
    pl.semaphore_wait(barrier, N_VIR + N_OCC - 2)
    lax.fori_loop(1, N_OCC, pass_on, 0)

    def send(slot, send_sem, recv_sem, peer):
        return pltpu.make_async_remote_copy(
            src_ref=full.at[slot], dst_ref=full.at[slot], send_sem=send_sem, recv_sem=recv_sem,
            device_id={"vir": peer}, device_id_type=MESH)

    sends = []

    def go(copy):
        copy.start()
        sends.append(copy)

    loads[0].wait()
    for dz in reversed(Z_ORDER):
        go(send(me, z_send.at[dz], z_recv.at[dz], ((z + dz) % N_Z) * 4 + x * 2 + c))
    go(send(me, x_send.at[0], x_recv.at[0], x_peer))
    go(send(me, c_send.at[0], c_recv.at[0], c_peer))

    def from_x(dz):
        slot = ((z - dz + N_Z) % N_Z) * 4 + (1 - x) * 2 + c
        send(slot, x_send.at[dz], x_recv.at[dz], x_peer).wait_recv()
        go(send(slot, d_send.at[dz], d_recv.at[dz], c_peer))

    def mask_amps():
        loads[1].wait()
        loads[2].wait()
        wide = one_hot(N_VIR, V, lambda r, c: r == c // VB)
        row = amask[pl.ds(me, 1), :].astype(F32).astype(BF16)
        keep = jnp.dot(jnp.broadcast_to(row, (8, N_VIR)), wide, preferred_element_type=F32)[:1].astype(BF16)

        def mask_one(n, carry):
            i, j = n // NO, n % NO
            masked[i, pl.ds(j * VB, VB), :] = amps[i, j] * keep
            return carry

        lax.fori_loop(0, 2 * NO, mask_one, 0, unroll=8)

    def make_holes():
        loads[3].wait()
        loads[4].wait()
        spread = one_hot(NO, ROWS, lambda r, c: r == c // VB)
        g_wide = lax.dot_general(g[...], spread, (((0,), (0,)), ((), ())), preferred_element_type=F32).astype(BF16)
        pick = one_hot(ROWS, NO, lambda r, c: r // VB == c)
        kron = jnp.dot(pick, g_wide, preferred_element_type=F32)
        same = lax.broadcasted_iota(jnp.int32, kron.shape, 0) % VB == lax.broadcasted_iota(jnp.int32, kron.shape, 1) % VB
        holes[...] = jnp.where(same, kron, 0.0).astype(BF16)
        tall = one_hot(V, N_VIR, lambda r, c: r // VB == c)
        tall_mask[...] = jnp.dot(tall, imask[...].astype(F32).astype(BF16), preferred_element_type=F32).astype(BF16)

    def add_holes(i):
        def tile(n, carry):
            cols = pl.ds(pl.multiple_of(n * 128, 128), 128)
            part = jnp.dot(holes[...], masked[i, :, cols], preferred_element_type=F32)
            num_ref[i, :, :, cols] = part.reshape(NO, VB, 128)
            return carry

        lax.fori_loop(0, N_PAIR, tile, 0)

    work = {1: mask_amps, 2: make_holes, 3: lambda: add_holes(0), 4: lambda: add_holes(1)}
    before = 0
    for dz in Z_ORDER:
        slot = ((z - dz + N_Z) % N_Z) * 4 + x * 2 + c
        send(slot, z_send.at[dz], z_recv.at[dz], x_peer).wait_recv()
        go(send(slot, x_send.at[dz], x_recv.at[dz], x_peer))
        go(send(slot, c_send.at[dz], c_recv.at[dz], c_peer))
        from_x(before)
        before = dz
        if dz in work:
            work[dz]()
    from_x(before)
    for dz in range(N_Z):
        slot = ((z - dz + N_Z) % N_Z) * 4 + x * 2 + (1 - c)
        send(slot, c_send.at[dz], c_recv.at[dz], c_peer).wait_recv()
        slot = ((z - dz + N_Z) % N_Z) * 4 + (1 - x) * 2 + (1 - c)
        send(slot, d_send.at[dz], d_recv.at[dz], c_peer).wait_recv()

    low = lax.broadcasted_iota(jnp.int32, (8, 8, 128), 2) < 64

    def make_tiles(q):
        cols = pl.ds(pl.multiple_of(q * 128, 128), 128)
        wide = one_hot(N_VIR, 128, lambda r, c: r == q * 8 + c // VB)
        w = full[:, :, cols].reshape(V, 128) * jnp.dot(tall_mask[...], wide, preferred_element_type=F32).astype(BF16)

        def ladder(i, carry):
            part = jnp.dot(masked[i], w, preferred_element_type=F32)
            num_ref[i, :, :, cols] += part.reshape(NO, VB, 128)
            return carry

        lax.fori_loop(0, 2, ladder, 0)

        def pack(p, carry):
            slabs = [num_ref[i, pl.ds(4 * p + 2 * h, 2), :, cols].reshape(2 * VB, 128) for h in (0, 1) for i in (0, 1)]
            turned = jnp.concatenate(slabs, axis=0).T.reshape(8, 2, 8, 128)
            top, bottom = turned[:, 0], turned[:, 1]
            tiles[pl.ds(2 * p * N_VIR + q * 8, 8)] = jnp.where(low, top, pltpu.roll(bottom, 64, 2)).astype(BF16)
            tiles[pl.ds((2 * p + 1) * N_VIR + q * 8, 8)] = jnp.where(low, pltpu.roll(top, 64, 2), bottom).astype(BF16)
            return carry

        lax.fori_loop(0, N_OCC // 2, pack, 0)

    def post(to_occ, to_vir, sem):
        pltpu.make_async_remote_copy(
            src_ref=tiles.at[to_occ * N_VIR + to_vir], dst_ref=arrived.at[flat], send_sem=out_sem, recv_sem=tile_sem.at[sem],
            device_id=(to_occ, to_vir), device_id_type=MESH).start()

    def lane(to_z, k):
        return to_z * 4 + ((x + k // 2) % 2) * 2 + (c + k) % 2

    for group in PAIR_ORDER:
        for dq in group:
            make_tiles((zp + dq) % N_PAIR)
        if group[0] == 3:
            pl.semaphore_wait(entered, N_OCC - 1)
        if group[0]:
            to_zs = [((zp + dq) % N_PAIR) * 2 + e for e in (0, 1) for dq in group]

            def post_pair(m, carry):
                to_occ = (occ + 8 + m * 5 + m // 16) % N_OCC
                for n, to_z in enumerate(to_zs):
                    post((to_occ + 4 * n) % N_OCC, lane(to_z, m // 16 + n), (to_z - z + N_Z) % N_Z)
                return carry

            lax.fori_loop(0, 64, post_pair, 0)
        else:
            other = zp * 2 + 1 - odd

            def post_near(m, carry):
                to_occ = (occ + 8 + m * 5 + m // 16) % N_OCC
                post(to_occ, lane(other, m // 16), (other - z + N_Z) % N_Z)
                return carry

            lax.fori_loop(0, 64, post_near, 0)

            def post_here(s, carry):
                for k in range(4):
                    post((occ + s) % N_OCC, lane(z, k), 0)
                return carry

            lax.fori_loop(1, N_OCC, post_here, 0)
            for k in range(1, 4):
                post(occ, lane(z, k), 0)
            own = pltpu.make_async_copy(tiles.at[flat], arrived.at[flat], own_sem)
            own.start()
            own.wait()

    for copy in sends:
        copy.wait_send()

    def wait_tiles(dz, count):
        part = arrived.at[pl.ds(0, count)]
        pltpu.make_async_copy(part, part, tile_sem.at[dz]).wait()

    chunk = lax.broadcasted_iota(jnp.int32, (8, 128), 1) // VB

    def add_mirror(q):
        cols = pl.ds(pl.multiple_of(q * 128, 128), 128)

        def one(source, carry):
            parts = [arrived[source * N_VIR + q * 8 + t].astype(F32) for t in range(8)]
            for k in (1, 2, 4):
                keep = (chunk // k) % 2 == 0
                for t in range(8):
                    if t & k == 0:
                        a, b = parts[t], parts[t + k]
                        parts[t] = jnp.where(keep, a, pltpu.roll(b, VB * k, 1))
                        parts[t + k] = jnp.where(keep, pltpu.roll(a, 128 - VB * k, 1), b)
            for n in range(8):
                half, i, jj = n // 4, (n // 2) % 2, n % 2
                num_ref[jj, 2 * source + i, half * 8 : half * 8 + 8, cols] += parts[n]
            return carry

        lax.fori_loop(0, N_OCC, one, 0, unroll=2)

    for group in PAIR_ORDER:
        for dq in group:
            q = (zp - dq + N_PAIR) % N_PAIR
            if dq:
                for e in (0, 1):
                    wait_tiles((z - (2 * q + e) + N_Z) % N_Z, 64)
            else:
                wait_tiles((z - (zp * 2 + 1 - odd) + N_Z) % N_Z, 64)
                wait_tiles(0, 63)
            add_mirror(q)

    others = tiles.at[pl.ds(0, N_DEV - 1)]
    pltpu.make_async_copy(others, others, out_sem).wait()


def local(amplitudes, integrals, occ_fock, amp_mask, int_mask, occ_energy, vir_energy):
    sem = pltpu.SemaphoreType.DMA
    total = pl.pallas_call(
        kernel,
        out_shape=jax.ShapeDtypeStruct(amplitudes.shape, F32),
        in_specs=[IN_HBM] * 5,
        out_specs=IN_VMEM,
        scratch_shapes=[
            pltpu.VMEM(amplitudes.shape, BF16),
            pltpu.VMEM(occ_fock.shape, BF16),
            pltpu.VMEM(amp_mask.shape, jnp.int32),
            pltpu.VMEM(int_mask.shape, jnp.int32),
            pltpu.VMEM((N_VIR, VB, V), BF16),
            pltpu.VMEM((2, ROWS, V), BF16),
            pltpu.VMEM((ROWS, ROWS), BF16),
            pltpu.VMEM((V, N_VIR), BF16),
            pltpu.VMEM((N_DEV, 8, 128), BF16),
            pltpu.VMEM((N_DEV, 8, 128), BF16),
            sem((5,)),
        ]
        + [sem((N_Z,))] * 8
        + [pltpu.SemaphoreType.REGULAR, sem, sem((N_Z,)), sem],
        compiler_params=pltpu.CompilerParams(collective_id=0, has_side_effects=True, vmem_limit_bytes=60 * 2**20),
        name="residual",
    )(amplitudes, integrals, occ_fock, amp_mask, int_mask)
    vir_here = lax.dynamic_slice_in_dim(vir_energy, lax.axis_index("vir") * VB, VB, 0)
    occ_here = lax.dynamic_slice_in_dim(occ_energy, lax.axis_index("occ") * 2, 2, 0)
    denominator = (
        vir_here[None, None, :, None]
        + vir_energy[None, None, None, :]
        - occ_here[:, None, None, None]
        - occ_energy[None, :, None, None]
    )
    return total / denominator


def solution(mesh):
    in_specs = (P("occ", None, "vir", None), P("vir", None), P(), P(), P(), P(), P())
    out_specs = P("occ", None, "vir", None)
    return jax.shard_map(local, mesh=mesh, in_specs=in_specs, out_specs=out_specs, check_vma=False)
```

```python
import jax
import jax.numpy as jnp
from jax import lax
from jax.experimental import pallas as pl
from jax.experimental.pallas import tpu as pltpu
from jax.sharding import PartitionSpec as P

VB = 16
NO = 32
V = 768
N_OCC = 16
N_VIR = 48
N_Z = 12
N_DEV = N_OCC * N_VIR
N_PAIR = N_Z // 2
ROWS = NO * VB
MESH = pl.DeviceIdType.MESH
F32, BF16 = jnp.float32, jnp.bfloat16
IN_HBM = pl.BlockSpec(memory_space=pl.ANY)

PAIR_ORDER = ((3,), (2, 4), (1, 5), (0,))


def one_hot(rows, cols, hit):
    r = lax.broadcasted_iota(jnp.int32, (rows, cols), 0)
    c = lax.broadcasted_iota(jnp.int32, (rows, cols), 1)
    return jnp.where(hit(r, c), 1.0, 0.0).astype(BF16)


def near(n):
    return (n % 2) * ((n + 1) // 2) + (1 - n % 2) * ((N_Z - n // 2) % N_Z)


def kernel(
    amps_hbm, w_hbm, g_hbm, amask_hbm, imask_hbm, vir_hbm, occ_energy, out_hbm,
    num_ref, amps, g, amask, imask, energies, sums, twice, full, masked, holes, tall_mask, tiles, arrived,
    in_sem, w_sem, put_sem, w_send, z_recv, x_recv, c_recv, d_recv, entered, out_sem, tile_sem, own_sem, done_sem,
):
    occ, me = lax.axis_index("occ"), lax.axis_index("vir")
    flat = occ * N_VIR + me
    z, x, c = me // 4, (me // 2) % 2, me % 2
    zp, odd = z // 2, z % 2
    x_peer, c_peer = z * 4 + (1 - x) * 2 + c, z * 4 + x * 2 + (1 - c)

    for q in range(2 * N_PAIR):
        cols = slice((q % N_PAIR) * 128, (q % N_PAIR) * 128 + 128)
        pltpu.make_async_copy(w_hbm.at[:, cols], twice.at[q], w_sem).start()
    pairs = ((amps_hbm, amps), (amask_hbm, amask), (g_hbm, g), (imask_hbm, imask), (vir_hbm, energies))
    loads = [pltpu.make_async_copy(src, dst, in_sem.at[n]) for n, (src, dst) in enumerate(pairs)]
    for load in loads:
        load.start()

    barrier = pltpu.get_barrier_semaphore()

    def greet_vir(s, carry):
        pl.semaphore_signal(barrier, inc=1, device_id=(occ, (me + s) % N_VIR), device_id_type=MESH)
        return carry

    def greet_occ(s, carry):
        pl.semaphore_signal(barrier, inc=1, device_id=((occ + s) % N_OCC, me), device_id_type=MESH)
        return carry

    def pass_on(s, carry):
        pl.semaphore_signal(entered, inc=1, device_id=((occ + s) % N_OCC, me), device_id_type=MESH)
        return carry

    lax.fori_loop(1, N_VIR, greet_vir, 0)
    lax.fori_loop(1, N_OCC, greet_occ, 0)

    def mask_amps():
        loads[0].wait()
        loads[1].wait()
        wide = one_hot(N_VIR, V, lambda r, c: r == c // VB)
        row = amask[pl.ds(me, 1), :].astype(F32).astype(BF16)
        keep = jnp.dot(jnp.broadcast_to(row, (8, N_VIR)), wide, preferred_element_type=F32)[:1].astype(BF16)

        def mask_one(n, carry):
            i, j = n // NO, n % NO
            masked[i, pl.ds(j * VB, VB), :] = amps[i, j] * keep
            return carry

        lax.fori_loop(0, 2 * NO, mask_one, 0, unroll=8)

    def make_holes():
        loads[2].wait()
        loads[3].wait()
        spread = one_hot(NO, ROWS, lambda r, c: r == c // VB)
        g_wide = lax.dot_general(g[...], spread, (((0,), (0,)), ((), ())), preferred_element_type=F32).astype(BF16)
        pick = one_hot(ROWS, NO, lambda r, c: r // VB == c)
        kron = jnp.dot(pick, g_wide, preferred_element_type=F32)
        same = lax.broadcasted_iota(jnp.int32, kron.shape, 0) % VB == lax.broadcasted_iota(jnp.int32, kron.shape, 1) % VB
        holes[...] = jnp.where(same, kron, 0.0).astype(BF16)
        tall = one_hot(V, N_VIR, lambda r, c: r // VB == c)
        tall_mask[...] = jnp.dot(tall, imask[...].astype(F32).astype(BF16), preferred_element_type=F32).astype(BF16)

    def add_holes(i):
        def tile(n, carry):
            cols = pl.ds(pl.multiple_of(n * 128, 128), 128)
            part = jnp.dot(holes[...], masked[i, :, cols], preferred_element_type=F32)
            num_ref[i, :, :, cols] = part.reshape(NO, VB, 128)
            return carry

        lax.fori_loop(0, N_PAIR, tile, 0)

    def add_energies():
        loads[4].wait()
        row = jnp.broadcast_to(energies[...].reshape(1, V), (VB, V))
        here = me * VB + lax.broadcasted_iota(jnp.int32, (VB, V), 0) == lax.broadcasted_iota(jnp.int32, (VB, V), 1)
        sums[...] = row + jnp.sum(jnp.where(here, row, 0.0), axis=1, keepdims=True)

    mask_amps()
    make_holes()
    add_holes(0)
    add_holes(1)
    add_energies()
    pltpu.make_async_copy(twice, twice, w_sem).wait()

    pl.semaphore_wait(barrier, N_VIR + N_OCC - 2)
    lax.fori_loop(1, N_OCC, pass_on, 0)

    def part(ref, first, stage):
        return ref.at[first] if stage == 0 else ref.at[pl.ds(first + 1, N_PAIR - 1)]

    def own_to(peer, stage, recv_sem):
        first = (peer // 8 + 3) % N_PAIR
        pltpu.make_async_remote_copy(
            src_ref=part(twice, first, stage), dst_ref=part(full.at[me], 0, stage), send_sem=w_send, recv_sem=recv_sem,
            device_id={"vir": peer}, device_id_type=MESH).start()

    def relay(slot, stage, recv_sem, peer):
        here = part(full.at[slot], 0, stage)
        return pltpu.make_async_remote_copy(
            src_ref=here, dst_ref=here, send_sem=w_send, recv_sem=recv_sem,
            device_id={"vir": peer}, device_id_type=MESH)

    put = pltpu.make_async_copy(twice.at[pl.ds((zp + 3) % N_PAIR, N_PAIR)], full.at[me], put_sem)
    put.start()
    for stage in (0, 1):

        def own_z(n, carry):
            dz = near(N_Z - n)
            own_to(((z + dz) % N_Z) * 4 + x * 2 + c, stage, z_recv.at[stage * N_Z + dz])
            return carry

        lax.fori_loop(1, N_Z, own_z, 0)
        own_to(x_peer, stage, x_recv.at[stage * N_Z])
        own_to(c_peer, stage, c_recv.at[stage * N_Z])

    def gather_stage(stage):
        def from_x(dz):
            slot = ((z - dz + N_Z) % N_Z) * 4 + (1 - x) * 2 + c
            relay(slot, stage, x_recv.at[stage * N_Z + dz], x_peer).wait_recv()
            relay(slot, stage, d_recv.at[stage * N_Z + dz], c_peer).start()

        def from_z(n, carry):
            dz = near(n)
            slot = ((z - dz + N_Z) % N_Z) * 4 + x * 2 + c
            relay(slot, stage, z_recv.at[stage * N_Z + dz], x_peer).wait_recv()
            relay(slot, stage, x_recv.at[stage * N_Z + dz], x_peer).start()
            relay(slot, stage, c_recv.at[stage * N_Z + dz], c_peer).start()
            from_x(near(n - 1))
            return carry

        def from_core(dz, carry):
            slot = ((z - dz + N_Z) % N_Z) * 4 + x * 2 + (1 - c)
            relay(slot, stage, c_recv.at[stage * N_Z + dz], c_peer).wait_recv()
            slot = ((z - dz + N_Z) % N_Z) * 4 + (1 - x) * 2 + (1 - c)
            relay(slot, stage, d_recv.at[stage * N_Z + dz], c_peer).wait_recv()
            return carry

        lax.fori_loop(1, N_Z, from_z, 0)
        from_x(6)
        lax.fori_loop(0, N_Z, from_core, 0)

    low = lax.broadcasted_iota(jnp.int32, (8, 8, 128), 2) < 64

    def make_tiles(dq):
        q = (zp + dq) % N_PAIR
        cols = pl.ds(pl.multiple_of(q * 128, 128), 128)
        wide = one_hot(N_VIR, 128, lambda r, c: r == q * 8 + c // VB)
        w = full[:, (dq + 3) % N_PAIR].reshape(V, 128) * jnp.dot(tall_mask[...], wide, preferred_element_type=F32).astype(BF16)

        def ladder(i, carry):
            part = jnp.dot(masked[i], w, preferred_element_type=F32)
            num_ref[i, :, :, cols] += part.reshape(NO, VB, 128)
            return carry

        lax.fori_loop(0, 2, ladder, 0)

        def pack(p, carry):
            slabs = [num_ref[i, pl.ds(4 * p + 2 * h, 2), :, cols].reshape(2 * VB, 128) for h in (0, 1) for i in (0, 1)]
            turned = jnp.concatenate(slabs, axis=0).T.reshape(8, 2, 8, 128)
            top, bottom = turned[:, 0], turned[:, 1]
            tiles[pl.ds(2 * p * N_VIR + q * 8, 8)] = jnp.where(low, top, pltpu.roll(bottom, 64, 2)).astype(BF16)
            tiles[pl.ds((2 * p + 1) * N_VIR + q * 8, 8)] = jnp.where(low, pltpu.roll(top, 64, 2), bottom).astype(BF16)
            return carry

        lax.fori_loop(0, N_OCC // 2, pack, 0)

    def post(to_occ, to_vir, sem):
        pltpu.make_async_remote_copy(
            src_ref=tiles.at[to_occ * N_VIR + to_vir], dst_ref=arrived.at[flat], send_sem=out_sem, recv_sem=tile_sem.at[sem],
            device_id=(to_occ, to_vir), device_id_type=MESH).start()

    def lane(to_z, k):
        return to_z * 4 + ((x + k // 2) % 2) * 2 + (c + k) % 2

    for group in PAIR_ORDER:
        if group[0] == 3:
            put.wait()
            gather_stage(0)
        elif group[0] == 2:
            gather_stage(1)
        for dq in group:
            make_tiles(dq)
        if group[0] == 3:
            pl.semaphore_wait(entered, N_OCC - 1)
        if group[0]:
            to_zs = [((zp + dq) % N_PAIR) * 2 + e for e in (0, 1) for dq in group]

            def post_pair(m, carry):
                to_occ = (occ + 8 + m * 5 + m // 16) % N_OCC
                for n, to_z in enumerate(to_zs):
                    post((to_occ + 4 * n) % N_OCC, lane(to_z, m // 16 + n), (to_z - z + N_Z) % N_Z)
                return carry

            lax.fori_loop(0, 64, post_pair, 0)
        else:
            other = zp * 2 + 1 - odd

            def post_near(m, carry):
                to_occ = (occ + 8 + m * 5 + m // 16) % N_OCC
                post(to_occ, lane(other, m // 16), (other - z + N_Z) % N_Z)
                return carry

            lax.fori_loop(0, 64, post_near, 0)

            def post_here(s, carry):
                for k in range(4):
                    post((occ + s) % N_OCC, lane(z, k), 0)
                return carry

            lax.fori_loop(1, N_OCC, post_here, 0)
            for k in range(1, 4):
                post(occ, lane(z, k), 0)
            own = pltpu.make_async_copy(tiles.at[flat], arrived.at[flat], own_sem)
            own.start()
            own.wait()

    def wait_tiles(dz, count):
        part = arrived.at[pl.ds(0, count)]
        pltpu.make_async_copy(part, part, tile_sem.at[dz]).wait()

    chunk = lax.broadcasted_iota(jnp.int32, (8, 128), 1) // VB

    def add_mirror(q):
        cols = pl.ds(pl.multiple_of(q * 128, 128), 128)

        def one(source, carry):
            parts = [arrived[source * N_VIR + q * 8 + t].astype(F32) for t in range(8)]
            for k in (1, 2, 4):
                keep = (chunk // k) % 2 == 0
                for t in range(8):
                    if t & k == 0:
                        a, b = parts[t], parts[t + k]
                        parts[t] = jnp.where(keep, a, pltpu.roll(b, VB * k, 1))
                        parts[t + k] = jnp.where(keep, pltpu.roll(a, 128 - VB * k, 1), b)
            for n in range(8):
                half, i, jj = n // 4, (n // 2) % 2, n % 2
                rows = slice(half * 8, half * 8 + 8)
                total = num_ref[jj, 2 * source + i, rows, cols] + parts[n]
                energy = occ_energy[2 * occ + jj] + occ_energy[2 * source + i]
                num_ref[jj, 2 * source + i, rows, cols] = total / (sums[rows, cols] - energy)
            return carry

        lax.fori_loop(0, N_OCC, one, 0, unroll=2)

    def write(q):
        cols = pl.ds(pl.multiple_of(q * 128, 128), 128)
        return pltpu.make_async_copy(num_ref.at[:, :, :, cols], out_hbm.at[:, :, :, cols], done_sem.at[q])

    for group in PAIR_ORDER:
        for dq in group:
            q = (zp - dq + N_PAIR) % N_PAIR
            if dq:
                for e in (0, 1):
                    wait_tiles((z - (2 * q + e) + N_Z) % N_Z, 64)
            else:
                wait_tiles((z - (zp * 2 + 1 - odd) + N_Z) % N_Z, 64)
                wait_tiles(0, 63)
            add_mirror(q)
            write(q).start()

    for q in range(N_PAIR):
        write(q).wait()
    most = full.at[pl.ds(0, N_VIR - 1)]
    pltpu.make_async_copy(most, most, w_send).wait()
    others = tiles.at[pl.ds(0, N_DEV - 1)]
    pltpu.make_async_copy(others, others, out_sem).wait()


def copy_kernel(x_ref, o_ref):
    o_ref[...] = x_ref[...]


def local(amplitudes, integrals, occ_fock, amp_mask, int_mask, occ_energy, vir_energy):
    sem = pltpu.SemaphoreType.DMA
    stages = sem((2 * N_Z,))
    update = pl.pallas_call(
        kernel,
        out_shape=jax.ShapeDtypeStruct(amplitudes.shape, F32),
        in_specs=[IN_HBM] * 6 + [pl.BlockSpec(memory_space=pltpu.SMEM)],
        out_specs=IN_HBM,
        scratch_shapes=[
            pltpu.VMEM(amplitudes.shape, F32),
            pltpu.VMEM(amplitudes.shape, BF16),
            pltpu.VMEM(occ_fock.shape, BF16),
            pltpu.VMEM(amp_mask.shape, jnp.int32),
            pltpu.VMEM(int_mask.shape, jnp.int32),
            pltpu.VMEM(vir_energy.shape, F32),
            pltpu.VMEM((VB, V), F32),
            pltpu.VMEM((2 * N_PAIR, VB, 128), BF16),
            pltpu.VMEM((N_VIR, N_PAIR, VB, 128), BF16),
            pltpu.VMEM((2, ROWS, V), BF16),
            pltpu.VMEM((ROWS, ROWS), BF16),
            pltpu.VMEM((V, N_VIR), BF16),
            pltpu.VMEM((N_DEV, 8, 128), BF16),
            pltpu.VMEM((N_DEV, 8, 128), BF16),
            sem((5,)), sem, sem, sem, stages, stages, stages, stages,
            pltpu.SemaphoreType.REGULAR, sem, sem((N_Z,)), sem, sem((N_PAIR,)),
        ],
        compiler_params=pltpu.CompilerParams(collective_id=0, has_side_effects=True, vmem_limit_bytes=60 * 2**20),
        name="residual",
    )(amplitudes, integrals, occ_fock, amp_mask, int_mask, vir_energy, occ_energy)
    block = pl.BlockSpec((2, 4, VB, V), lambda s: (0, s, 0, 0))
    return pl.pallas_call(
        copy_kernel,
        out_shape=jax.ShapeDtypeStruct(amplitudes.shape, F32),
        grid=(NO // 4,),
        in_specs=[block],
        out_specs=block,
        name="place",
    )(update)


def solution(mesh):
    in_specs = (P("occ", None, "vir", None), P("vir", None), P(), P(), P(), P(), P())
    out_specs = P("occ", None, "vir", None)
    return jax.shard_map(local, mesh=mesh, in_specs=in_specs, out_specs=out_specs, check_vma=False)
```

```python
import jax
import jax.numpy as jnp
from jax import lax
from jax.experimental import pallas as pl
from jax.experimental.pallas import tpu as pltpu
from jax.sharding import PartitionSpec as P

VB = 16
NO = 32
V = 768
N_OCC = 16
N_VIR = 48
N_Z = 12
N_DEV = N_OCC * N_VIR
N_PAIR = N_Z // 2
ROWS = NO * VB
MESH = pl.DeviceIdType.MESH
F32, BF16 = jnp.float32, jnp.bfloat16
IN_HBM = pl.BlockSpec(memory_space=pl.ANY)

PAIR_ORDER = ((3,), (2, 4), (1, 5), (0,))


def one_hot(rows, cols, hit):
    r = lax.broadcasted_iota(jnp.int32, (rows, cols), 0)
    c = lax.broadcasted_iota(jnp.int32, (rows, cols), 1)
    return jnp.where(hit(r, c), 1.0, 0.0).astype(BF16)


def near(n):
    return (n % 2) * ((n + 1) // 2) + (1 - n % 2) * ((N_Z - n // 2) % N_Z)


def kernel(
    amps_hbm, w_hbm, g_hbm, amask_hbm, imask_hbm, vir_hbm, occ_energy, out_hbm,
    num_ref, amps, g, amask, imask, energies, sums, twice, full, masked, holes, tall_mask, tiles, arrived,
    in_sem, w_sem, put_sem, w_send, z_recv, x_recv, c_recv, d_recv, entered, out_sem, tile_sem, own_sem, done_sem,
):
    occ, me = lax.axis_index("occ"), lax.axis_index("vir")
    flat = occ * N_VIR + me
    z, x, c = me // 4, (me // 2) % 2, me % 2
    zp, odd = z // 2, z % 2
    x_peer, c_peer = z * 4 + (1 - x) * 2 + c, z * 4 + x * 2 + (1 - c)

    for q in range(2 * N_PAIR):
        cols = slice((q % N_PAIR) * 128, (q % N_PAIR) * 128 + 128)
        pltpu.make_async_copy(w_hbm.at[:, cols], twice.at[q], w_sem).start()
    pairs = ((amps_hbm, amps), (amask_hbm, amask), (g_hbm, g), (imask_hbm, imask), (vir_hbm, energies))
    loads = [pltpu.make_async_copy(src, dst, in_sem.at[n]) for n, (src, dst) in enumerate(pairs)]
    for load in loads:
        load.start()

    barrier = pltpu.get_barrier_semaphore()

    def greet_vir(s, carry):
        pl.semaphore_signal(barrier, inc=1, device_id=(occ, (me + s) % N_VIR), device_id_type=MESH)
        return carry

    def greet_occ(s, carry):
        pl.semaphore_signal(barrier, inc=1, device_id=((occ + s) % N_OCC, me), device_id_type=MESH)
        return carry

    def pass_on(s, carry):
        pl.semaphore_signal(entered, inc=1, device_id=((occ + s) % N_OCC, me), device_id_type=MESH)
        return carry

    lax.fori_loop(1, N_VIR, greet_vir, 0)
    lax.fori_loop(1, N_OCC, greet_occ, 0)

    def mask_amps():
        loads[0].wait()
        loads[1].wait()
        wide = one_hot(N_VIR, V, lambda r, c: r == c // VB)
        row = amask[pl.ds(me, 1), :].astype(F32).astype(BF16)
        keep = jnp.dot(jnp.broadcast_to(row, (8, N_VIR)), wide, preferred_element_type=F32)[:1].astype(BF16)

        def mask_one(n, carry):
            i, j = n // NO, n % NO
            masked[i, pl.ds(j * VB, VB), :] = amps[i, j] * keep
            return carry

        lax.fori_loop(0, 2 * NO, mask_one, 0, unroll=8)

    def make_holes():
        loads[2].wait()
        loads[3].wait()
        spread = one_hot(NO, ROWS, lambda r, c: r == c // VB)
        g_wide = lax.dot_general(g[...], spread, (((0,), (0,)), ((), ())), preferred_element_type=F32).astype(BF16)
        pick = one_hot(ROWS, NO, lambda r, c: r // VB == c)
        kron = jnp.dot(pick, g_wide, preferred_element_type=F32)
        same = lax.broadcasted_iota(jnp.int32, kron.shape, 0) % VB == lax.broadcasted_iota(jnp.int32, kron.shape, 1) % VB
        holes[...] = jnp.where(same, kron, 0.0).astype(BF16)
        tall = one_hot(V, N_VIR, lambda r, c: r // VB == c)
        tall_mask[...] = jnp.dot(tall, imask[...].astype(F32).astype(BF16), preferred_element_type=F32).astype(BF16)

    def add_holes(i):
        def tile(n, carry):
            cols = pl.ds(pl.multiple_of(n * 256, 256), 256)
            part = jnp.dot(holes[...], masked[i, :, cols], preferred_element_type=F32)
            num_ref[i, :, :, cols] = part.reshape(NO, VB, 256)
            return carry

        lax.fori_loop(0, N_PAIR // 2, tile, 0)

    def add_energies():
        loads[4].wait()
        row = jnp.broadcast_to(energies[...].reshape(1, V), (VB, V))
        here = me * VB + lax.broadcasted_iota(jnp.int32, (VB, V), 0) == lax.broadcasted_iota(jnp.int32, (VB, V), 1)
        sums[...] = row + jnp.sum(jnp.where(here, row, 0.0), axis=1, keepdims=True)

    mask_amps()
    make_holes()
    add_holes(0)
    add_holes(1)
    add_energies()
    pltpu.make_async_copy(twice, twice, w_sem).wait()

    pl.semaphore_wait(barrier, N_VIR + N_OCC - 2)
    lax.fori_loop(1, N_OCC, pass_on, 0)

    def part(ref, first, stage):
        return ref.at[first] if stage == 0 else ref.at[pl.ds(first + 1, N_PAIR - 1)]

    def own_to(peer, stage, recv_sem):
        first = (peer // 8 + 3) % N_PAIR
        pltpu.make_async_remote_copy(
            src_ref=part(twice, first, stage), dst_ref=part(full.at[me], 0, stage), send_sem=w_send, recv_sem=recv_sem,
            device_id={"vir": peer}, device_id_type=MESH).start()

    def relay(slot, stage, recv_sem, peer):
        here = part(full.at[slot], 0, stage)
        return pltpu.make_async_remote_copy(
            src_ref=here, dst_ref=here, send_sem=w_send, recv_sem=recv_sem,
            device_id={"vir": peer}, device_id_type=MESH)

    put = pltpu.make_async_copy(twice.at[pl.ds((zp + 3) % N_PAIR, N_PAIR)], full.at[me], put_sem)
    put.start()
    for stage in (0, 1):

        def own_z(n, carry):
            dz = near(n)
            own_to(((z + dz) % N_Z) * 4 + x * 2 + c, stage, z_recv.at[stage * N_Z + dz])
            return carry

        lax.fori_loop(1, N_Z, own_z, 0)
        own_to(x_peer, stage, x_recv.at[stage * N_Z])
        own_to(c_peer, stage, c_recv.at[stage * N_Z])

    def gather_stage(stage):
        def from_x(dz):
            slot = ((z - dz + N_Z) % N_Z) * 4 + (1 - x) * 2 + c
            relay(slot, stage, x_recv.at[stage * N_Z + dz], x_peer).wait_recv()
            relay(slot, stage, d_recv.at[stage * N_Z + dz], c_peer).start()

        def from_z(n, carry):
            dz = near(n)
            slot = ((z - dz + N_Z) % N_Z) * 4 + x * 2 + c
            relay(slot, stage, z_recv.at[stage * N_Z + dz], x_peer).wait_recv()
            relay(slot, stage, x_recv.at[stage * N_Z + dz], x_peer).start()
            relay(slot, stage, c_recv.at[stage * N_Z + dz], c_peer).start()
            from_x(near(n - 1))
            return carry

        def from_core(dz, carry):
            slot = ((z - dz + N_Z) % N_Z) * 4 + x * 2 + (1 - c)
            relay(slot, stage, c_recv.at[stage * N_Z + dz], c_peer).wait_recv()
            slot = ((z - dz + N_Z) % N_Z) * 4 + (1 - x) * 2 + (1 - c)
            relay(slot, stage, d_recv.at[stage * N_Z + dz], c_peer).wait_recv()
            return carry

        lax.fori_loop(1, N_Z, from_z, 0)
        from_x(6)
        lax.fori_loop(0, N_Z, from_core, 0)

    low = lax.broadcasted_iota(jnp.int32, (8, 8, 128), 2) < 64

    def make_tiles(dq):
        q = (zp + dq) % N_PAIR
        cols = pl.ds(pl.multiple_of(q * 128, 128), 128)
        wide = one_hot(N_VIR, 128, lambda r, c: r == q * 8 + c // VB)
        w = full[:, (dq + 3) % N_PAIR].reshape(V, 128) * jnp.dot(tall_mask[...], wide, preferred_element_type=F32).astype(BF16)

        def ladder(i, carry):
            part = jnp.dot(masked[i], w, preferred_element_type=F32)
            num_ref[i, :, :, cols] += part.reshape(NO, VB, 128)
            return carry

        lax.fori_loop(0, 2, ladder, 0)

        def pack(p, carry):
            slabs = [num_ref[i, pl.ds(4 * p + 2 * h, 2), :, cols].reshape(2 * VB, 128) for h in (0, 1) for i in (0, 1)]
            turned = jnp.concatenate(slabs, axis=0).T.reshape(8, 2, 8, 128)
            top, bottom = turned[:, 0], turned[:, 1]
            tiles[pl.ds(2 * p * N_VIR + q * 8, 8)] = jnp.where(low, top, pltpu.roll(bottom, 64, 2)).astype(BF16)
            tiles[pl.ds((2 * p + 1) * N_VIR + q * 8, 8)] = jnp.where(low, pltpu.roll(top, 64, 2), bottom).astype(BF16)
            return carry

        lax.fori_loop(0, N_OCC // 2, pack, 0)

    def post(to_occ, to_vir, sem):
        pltpu.make_async_remote_copy(
            src_ref=tiles.at[to_occ * N_VIR + to_vir], dst_ref=mine, send_sem=out_sem, recv_sem=sem,
            device_id=(to_occ, to_vir), device_id_type=MESH).start()

    mine = arrived.at[flat]
    peers = (me % 4, (1 - x) * 2 + c, x * 2 + (1 - c), (1 - x) * 2 + (1 - c))

    def post_all(to_zs):
        sems = [tile_sem.at[lax.rem(to_z - z + N_Z, N_Z)] for to_z in to_zs]

        for k in range(4):
            cols = [to_z * 4 + peers[(k + n) % 4] for n, to_z in enumerate(to_zs)]

            def row(s, carry):
                base = occ + s * 5 + 4 * k
                for n, col in enumerate(cols):
                    post(lax.rem(base + 4 * n, N_OCC), col, sems[n])
                return carry

            lax.fori_loop(0, N_OCC, row, 0, unroll=2)

    for group in PAIR_ORDER:
        if group[0] == 3:
            put.wait()
            gather_stage(0)
        elif group[0] == 2:
            gather_stage(1)
        for dq in group:
            make_tiles(dq)
        if group[0] == 3:
            pl.semaphore_wait(entered, N_OCC - 1)
        if group[0]:
            post_all([((zp + dq) % N_PAIR) * 2 + e for e in (0, 1) for dq in group])
        else:
            post_all([zp * 2 + 1 - odd])

            def post_here(s, carry):
                for peer in peers:
                    post(lax.rem(occ + s, N_OCC), z * 4 + peer, tile_sem.at[0])
                return carry

            lax.fori_loop(1, N_OCC, post_here, 0, unroll=3)
            for peer in peers[1:]:
                post(occ, z * 4 + peer, tile_sem.at[0])
            own = pltpu.make_async_copy(tiles.at[flat], mine, own_sem)
            own.start()
            own.wait()

    def wait_tiles(dz, count):
        part = arrived.at[pl.ds(0, count)]
        pltpu.make_async_copy(part, part, tile_sem.at[dz]).wait()

    chunk = lax.broadcasted_iota(jnp.int32, (8, 128), 1) // VB

    def add_mirror(q):
        cols = pl.ds(pl.multiple_of(q * 128, 128), 128)

        def one(source, carry):
            parts = [arrived[source * N_VIR + q * 8 + t].astype(F32) for t in range(8)]
            for k in (1, 2, 4):
                keep = (chunk // k) % 2 == 0
                for t in range(8):
                    if t & k == 0:
                        a, b = parts[t], parts[t + k]
                        parts[t] = jnp.where(keep, a, pltpu.roll(b, VB * k, 1))
                        parts[t + k] = jnp.where(keep, pltpu.roll(a, 128 - VB * k, 1), b)
            for n in range(8):
                half, i, jj = n // 4, (n // 2) % 2, n % 2
                rows = slice(half * 8, half * 8 + 8)
                total = num_ref[jj, 2 * source + i, rows, cols] + parts[n]
                energy = occ_energy[2 * occ + jj] + occ_energy[2 * source + i]
                num_ref[jj, 2 * source + i, rows, cols] = total / (sums[rows, cols] - energy)
            return carry

        lax.fori_loop(0, N_OCC, one, 0, unroll=2)

    def write(q):
        cols = pl.ds(pl.multiple_of(q * 128, 128), 128)
        return pltpu.make_async_copy(num_ref.at[:, :, :, cols], out_hbm.at[:, :, :, cols], done_sem.at[q])

    for group in PAIR_ORDER:
        for dq in group:
            q = (zp - dq + N_PAIR) % N_PAIR
            if dq:
                for e in (0, 1):
                    wait_tiles((z - (2 * q + e) + N_Z) % N_Z, 64)
            else:
                wait_tiles((z - (zp * 2 + 1 - odd) + N_Z) % N_Z, 64)
                wait_tiles(0, 63)
            add_mirror(q)
            write(q).start()

    for q in range(N_PAIR):
        write(q).wait()
    most = full.at[pl.ds(0, N_VIR - 1)]
    pltpu.make_async_copy(most, most, w_send).wait()
    others = tiles.at[pl.ds(0, N_DEV - 1)]
    pltpu.make_async_copy(others, others, out_sem).wait()


N_PIECE = 16


def copy_kernel(x_ref, o_ref, held, in_sem, out_sem):
    rows = 2 * NO // N_PIECE
    pieces = [(i, pl.ds(j, rows)) for i in (0, 1) for j in range(0, NO, rows)]
    ins = [pltpu.make_async_copy(x_ref.at[p], held.at[p], in_sem.at[n]) for n, p in enumerate(pieces)]
    outs = [pltpu.make_async_copy(held.at[p], o_ref.at[p], out_sem.at[n]) for n, p in enumerate(pieces)]
    for copy in ins:
        copy.start()
    for arrival, copy in zip(ins, outs):
        arrival.wait()
        copy.start()
    for copy in outs:
        copy.wait()


def local(amplitudes, integrals, occ_fock, amp_mask, int_mask, occ_energy, vir_energy):
    sem = pltpu.SemaphoreType.DMA
    stages = sem((2 * N_Z,))
    update = pl.pallas_call(
        kernel,
        out_shape=jax.ShapeDtypeStruct(amplitudes.shape, F32),
        in_specs=[IN_HBM] * 6 + [pl.BlockSpec(memory_space=pltpu.SMEM)],
        out_specs=IN_HBM,
        scratch_shapes=[
            pltpu.VMEM(amplitudes.shape, F32),
            pltpu.VMEM(amplitudes.shape, BF16),
            pltpu.VMEM(occ_fock.shape, BF16),
            pltpu.VMEM(amp_mask.shape, jnp.int32),
            pltpu.VMEM(int_mask.shape, jnp.int32),
            pltpu.VMEM(vir_energy.shape, F32),
            pltpu.VMEM((VB, V), F32),
            pltpu.VMEM((2 * N_PAIR, VB, 128), BF16),
            pltpu.VMEM((N_VIR, N_PAIR, VB, 128), BF16),
            pltpu.VMEM((2, ROWS, V), BF16),
            pltpu.VMEM((ROWS, ROWS), BF16),
            pltpu.VMEM((V, N_VIR), BF16),
            pltpu.VMEM((N_DEV, 8, 128), BF16),
            pltpu.VMEM((N_DEV, 8, 128), BF16),
            sem((5,)), sem, sem, sem, stages, stages, stages, stages,
            pltpu.SemaphoreType.REGULAR, sem, sem((N_Z,)), sem, sem((N_PAIR,)),
        ],
        compiler_params=pltpu.CompilerParams(collective_id=0, has_side_effects=True, vmem_limit_bytes=60 * 2**20),
        name="residual",
    )(amplitudes, integrals, occ_fock, amp_mask, int_mask, vir_energy, occ_energy)
    return pl.pallas_call(
        copy_kernel,
        out_shape=jax.ShapeDtypeStruct(amplitudes.shape, F32),
        in_specs=[IN_HBM],
        out_specs=IN_HBM,
        scratch_shapes=[pltpu.VMEM(amplitudes.shape, F32), sem((N_PIECE,)), sem((N_PIECE,))],
        name="place",
    )(update)


def solution(mesh):
    in_specs = (P("occ", None, "vir", None), P("vir", None), P(), P(), P(), P(), P())
    out_specs = P("occ", None, "vir", None)
    return jax.shard_map(local, mesh=mesh, in_specs=in_specs, out_specs=out_specs, check_vma=False)
```
